32 devices in a mesh: dp: 4 (over z), mp: 8 (over y, x, core).
Axes of the slice: x: 2, y: 2, z: 4, core: 2. Of those that a mesh axis runs over, the one named last changes fastest.
Arguments:
- tokens: bfloat16 [2048, 3072], P('dp', 'mp'), may hold values from -6 to 6
- w_first: bfloat16 [3072, 12288], P('dp', 'mp'), may hold values from -0.15625 to 0.15625
- w_second: bfloat16 [12288, 3072], P('mp', 'dp'), may hold values from -0.078125 to 0.078125
- cotangent: bfloat16 [2048, 3072], P('dp', 'mp'), may hold values from -1.5 to 1.5
Outputs:
- outputs: bfloat16 [2048, 3072], P('dp', 'mp')
- input_grad: bfloat16 [2048, 3072], P('dp', 'mp')
- first_grad: float32 [3072, 12288], P('dp', 'mp')
- second_grad: float32 [12288, 3072], P('mp', 'dp')
The draws below stay inside these ranges and needn't reach their ends.
All inputs are finite; a program needn't handle non-finite values.
Results may differ from the reference program's by a relative error of at most 0.018.
Values may be sent and summed in bfloat16 or wider, within the bound.
No kernel may reach another device: no remote copies, remote signals or barrier semaphores. Data moves between devices by JAX's collectives and lax.ppermute only.
A program may use at most 128 MiB of HBM per device.

```python
import jax
import jax.numpy as jnp
from jax import lax

D = 3072
FF = 12288
TOK_DEV = 512
TOKENS = 2048
N_DP = 4
N_MP = 8


def raised(entries, own_key, source, target, shards_of, factor):
    def block_of(dim):
        return (jnp.arange(entries.shape[dim]) // (entries.shape[dim] // shards_of)).reshape((-1,) + (1,) * (entries.ndim - 1 - dim))

    one_side = jax.random.permutation(own_key, shards_of)[block_of(target)]
    other_side = (block_of(target) + shards_of // 2) % shards_of
    return jnp.where((block_of(source) == one_side) | (block_of(source) == other_side), factor * entries, entries)


def steps_of(rng, extent, shards, least, high):
    def one(dim, parts):
        draws = jax.random.uniform(jax.random.fold_in(jax.random.fold_in(rng, 6), dim), (parts,), jnp.float32, least / len(shards), high / len(shards))
        return jnp.repeat(jnp.exp(draws), extent[dim] // parts).reshape((-1,) + (1,) * (len(extent) - dim - 1))

    factor_of = one(*shards[0])
    for cut in shards[1:]:
        factor_of = factor_of * one(*cut)
    return factor_of


def normal_values(own_key, dims, scale, limit, shards=(), dtype=jnp.bfloat16):
    entries = scale * jax.random.normal(own_key, dims, jnp.float32)
    if shards:
        entries = entries * steps_of(own_key, dims, shards, -0.22, 0.18)
    return jnp.clip(entries, -limit, limit).astype(dtype)


def heavy_noise(rng, shape, scale, most, cuts, heavy, kind=jnp.bfloat16):
    values = scale * jax.random.normal(rng, shape, jnp.float32)
    if cuts:
        values = values * steps_of(rng, shape, cuts, -0.22, 0.18)
    return jnp.clip(raised(values, jax.random.fold_in(rng, 3), *heavy), -most, most).astype(kind)


def setup_inputs(seed: int = 0) -> dict:
    arg_keys = jax.random.split(jax.random.key(seed), 5)
    tokens = normal_values(arg_keys[0], (TOKENS, D), 1.0, 6.0, ((0, 4), (1, 8)))
    w_first = heavy_noise(arg_keys[1], (D, FF), D ** -0.5, 0.15625, ((0, 4), (1, 8)), (1, 0, 8, 2.0))
    w_second = heavy_noise(arg_keys[2], (FF, D), FF ** -0.5, 0.078125, ((0, 8), (1, 4)), (0, 1, 8, 2.0))
    cotangent = normal_values(arg_keys[3], (TOKENS, D), 0.25, 1.5, ((0, 4), (1, 8)))
    return dict(tokens=tokens, w_first=w_first, w_second=w_second, cotangent=cotangent)


inv_root_two = 0.7071067811865476
inv_root_tau = 0.3989422804014327


def gelu_value(value):
    return 0.5 * value * (1.0 + lax.erf(value * inv_root_two))


def gelu_slope(value):
    return 0.5 * (1.0 + lax.erf(value * inv_root_two)) + value * jnp.exp(-0.5 * value * value) * inv_root_tau


def rounded(value):
    return lax.optimization_barrier(value.astype(jnp.bfloat16)).astype(jnp.float32)


def reference(tokens, w_first, w_second, cotangent):
    pre_act = jnp.dot(tokens, w_first, preferred_element_type=jnp.float32)
    activated = gelu_value(pre_act).astype(jnp.bfloat16)
    width = FF // N_MP
    act_blocks = activated.reshape(TOKENS, N_MP, width).transpose(1, 0, 2)
    second_blocks = w_second.reshape(N_MP, width, D)

    def add_output(total, pair):
        left, right = pair
        return total + rounded(jnp.dot(left, right, preferred_element_type=jnp.float32)), None

    summed, _ = lax.scan(add_output, jnp.zeros((TOKENS, D), jnp.float32), (act_blocks, second_blocks))
    outputs = summed.astype(jnp.bfloat16)
    back_pre = lax.dot_general(cotangent, w_second, (((1,), (1,)), ((), ())), preferred_element_type=jnp.float32)
    hidden_grad = (back_pre * gelu_slope(pre_act)).astype(jnp.bfloat16)

    def add_second(total, pair):
        left, right = pair
        return total + rounded(lax.dot_general(left, right, (((0,), (0,)), ((), ())), preferred_element_type=jnp.float32)), None

    second_grad, _ = lax.scan(add_second, jnp.zeros((FF, D), jnp.float32),
                              (activated.reshape(N_DP, TOK_DEV, FF), cotangent.reshape(N_DP, TOK_DEV, D)))
    first_grad, _ = lax.scan(add_second, jnp.zeros((D, FF), jnp.float32),
                             (tokens.reshape(N_DP, TOK_DEV, D), hidden_grad.reshape(N_DP, TOK_DEV, FF)))
    grad_blocks = hidden_grad.reshape(TOKENS, N_MP, width).transpose(1, 0, 2)
    first_blocks = w_first.reshape(D, N_MP, width).transpose(1, 0, 2)

    def add_input(total, pair):
        left, right = pair
        return total + rounded(lax.dot_general(left, right, (((1,), (1,)), ((), ())), preferred_element_type=jnp.float32)), None

    input_sum, _ = lax.scan(add_input, jnp.zeros((TOKENS, D), jnp.float32), (grad_blocks, first_blocks))
    input_grad = input_sum.astype(jnp.bfloat16)
    return outputs, input_grad, first_grad, second_grad
```

```python
import jax
import jax.numpy as jnp
from jax import lax
from jax.sharding import PartitionSpec as P

inv_root_two = 0.7071067811865476
inv_root_tau = 0.3989422804014327


def gelu_value(value):
    return 0.5 * value * (1.0 + lax.erf(value * inv_root_two))


def gelu_slope(value):
    return (
        0.5 * (1.0 + lax.erf(value * inv_root_two))
        + value * jnp.exp(-0.5 * value * value) * inv_root_tau
    )


def product(left, right, left_dim, right_dim):
    return lax.dot_general(
        left, right, (((left_dim,), (right_dim,)), ((), ())), preferred_element_type=jnp.float32
    )


def body(n_dp, n_mp):
    n_chips = n_mp // 2
    if n_chips != n_dp or n_dp & (n_dp - 1):
        raise ValueError("mesh shape")

    def move(value, dz, dm):
        if not dz and not dm:
            return value
        pairs = [
            (z * n_mp + m, (z ^ dz) * n_mp + (m ^ dm)) for z in range(n_dp) for m in range(n_mp)
        ]
        return lax.ppermute(value, ("dp", "mp"), pairs)

    z_masks = []
    span = n_dp
    while span > 1:
        z_masks.append(span - 1)
        span //= 2
    chip_bits = [1 << i for i in range(n_chips.bit_length() - 1)]

    def gather_z(own):
        blocks = {0: own}
        for mask in z_masks:
            blocks.update({j ^ mask: move(b, mask, 0) for j, b in list(blocks.items())})
        return blocks

    def reduce_z(blocks):
        blocks = dict(blocks)
        for mask in reversed(z_masks):
            for j in reach(mask):
                blocks[j] = blocks[j].astype(jnp.float32) + move(
                    blocks.pop(j ^ mask).astype(jnp.bfloat16), mask, 0
                ).astype(jnp.float32)
        return blocks[0]

    def reach(mask):
        known = [0]
        for earlier in z_masks:
            if earlier == mask:
                break
            known += [j ^ earlier for j in known]
        return known

    def gather_chips(own):
        if n_chips == 1:
            return {0: own}
        first = chip_bits[0]
        if len(chip_bits) == 1:
            return {0: own, first: move(own, 0, 2 * first)}
        second = chip_bits[1]
        half = own.shape[0] // 2
        a, b = move(own, 0, 2 * first), move(own, 0, 2 * second)
        upper = move(a[:half], 0, 2 * second)
        lower = move(b[half:], 0, 2 * first)
        blocks = {0: own, first: a, second: b, first ^ second: jnp.concatenate([upper, lower])}
        for bit in chip_bits[2:]:
            blocks.update({r ^ bit: move(b, 0, 2 * bit) for r, b in list(blocks.items())})
        return blocks

    def reduce_chips(blocks):
        blocks = {r: b for r, b in blocks.items()}

        def joined(kept, sent, bit):
            arrived = move(sent.astype(jnp.bfloat16), 0, 2 * bit)
            return kept.astype(jnp.float32) + arrived.astype(jnp.float32)

        for bit in reversed(chip_bits[2:]):
            for r in range(bit):
                blocks[r] = joined(blocks[r], blocks.pop(r ^ bit), bit)
        if len(chip_bits) == 1:
            return joined(blocks[0], blocks[1], 1)
        first, second = chip_bits[:2]
        far = blocks[first ^ second]
        half = far.shape[0] // 2
        to_second = jnp.concatenate(
            [joined(blocks[second][:half], far[:half], first).astype(jnp.bfloat16),
             blocks[second][half:].astype(jnp.bfloat16)]
        )
        to_first = jnp.concatenate(
            [blocks[first][:half].astype(jnp.bfloat16),
             joined(blocks[first][half:], far[half:], second).astype(jnp.bfloat16)]
        )
        return joined(joined(blocks[0], to_first, first), to_second, second)

    def shards(tokens, w_first, w_second, cotangent):
        z, m = lax.axis_index("dp"), lax.axis_index("mp")
        core = m & 1
        shift = z ^ (m >> 1)
        rows, width = tokens.shape
        units = w_first.shape[1] // n_dp
        places = range(n_dp)

        def spread(array, unit_dim):
            sizes = (units, width) if unit_dim == 0 else (width, units)
            full = (2 * units, n_chips * width) if unit_dim == 0 else (n_chips * width, 2 * units)
            result = jnp.zeros(full, array.dtype)
            for dz in places:
                for dm in range(2):
                    unit, feature = (z ^ dz) * units, (core ^ dm) * width
                    at = (unit, feature) if unit_dim == 0 else (feature, unit)
                    part = move(lax.dynamic_slice(array, at, sizes), dz, dm)
                    unit, feature = dm * units, (dz ^ shift) * width
                    at = (unit, feature) if unit_dim == 0 else (feature, unit)
                    result = lax.dynamic_update_slice(result, part, at)
            return result

        def unspread(array, unit_dim, shape):
            sizes = (units, width) if unit_dim == 0 else (width, units)
            result = jnp.zeros(shape, jnp.float32)
            for dz in places:
                for dm in range(2):
                    unit, feature = dm * units, (dz ^ shift) * width
                    at = (unit, feature) if unit_dim == 0 else (feature, unit)
                    part = move(lax.dynamic_slice(array, at, sizes), dz, dm)
                    unit, feature = (z ^ dz) * units, (core ^ dm) * width
                    at = (unit, feature) if unit_dim == 0 else (feature, unit)
                    result = lax.dynamic_update_slice(result, part.astype(jnp.float32), at)
            return result

        def gather(own):
            by_z = gather_z(own)
            return jnp.concatenate(
                [
                    jnp.concatenate([b for _, b in sorted(gather_chips(by_z[j]).items())], axis=1)
                    for j in places
                ]
            )

        def reduce(share):
            share = share.astype(jnp.bfloat16)
            by_z = {}
            for j in places:
                part = share[j * rows : (j + 1) * rows]
                by_z[j] = reduce_chips(
                    {r: part[:, r * width : (r + 1) * width] for r in range(n_chips)}
                )
            return reduce_z(by_z).astype(jnp.bfloat16)

        def over_cores(share):
            return share[:, :units] + move(share[:, units:], 0, 1)

        def both(half):
            return jnp.concatenate([half, move(half, 0, 1)], axis=1)

        inputs_all = gather(tokens)
        first = spread(w_first, 1)
        piece = gather(cotangent)
        second = spread(w_second, 0)
        pre_act = over_cores(product(inputs_all, first, 1, 0))
        activated = both(gelu_value(pre_act).astype(jnp.bfloat16))
        second_terms = product(activated, piece, 0, 0).astype(jnp.bfloat16)
        second_grad = unspread(second_terms, 0, w_second.shape)
        outputs = reduce(product(activated, second, 1, 0))
        back_pre = over_cores(product(piece, second, 1, 1))
        hidden_grad = both((back_pre * gelu_slope(pre_act)).astype(jnp.bfloat16))
        first_terms = product(inputs_all, hidden_grad, 0, 0).astype(jnp.bfloat16)
        first_grad = unspread(first_terms, 1, w_first.shape)
        input_grad = reduce(product(hidden_grad, first, 1, 1))
        return (outputs, input_grad, first_grad, second_grad)

    return shards


def solution(mesh):
    return jax.shard_map(
        body(mesh.shape["dp"], mesh.shape["mp"]),
        mesh=mesh,
        in_specs=(P("dp", "mp"), P("dp", "mp"), P("mp", "dp"), P("dp", "mp")),
        out_specs=(P("dp", "mp"), P("dp", "mp"), P("dp", "mp"), P("mp", "dp")),
        check_vma=False,
    )
```

```python
import jax
import jax.numpy as jnp
from jax import lax
from jax.experimental import pallas as pl
from jax.experimental.pallas import tpu as pltpu
from jax.sharding import PartitionSpec as P


inv_root_two = 0.7071067811865476
inv_root_tau = 0.3989422804014327


def gelu_value(value):
    return 0.5 * value * (1.0 + lax.erf(value * inv_root_two))


def gelu_slope(value):
    return (
        0.5 * (1.0 + lax.erf(value * inv_root_two))
        + value * jnp.exp(-0.5 * value * value) * inv_root_tau
    )


def product(left, right, left_dim, right_dim):
    return lax.dot_general(
        left, right, (((left_dim,), (right_dim,)), ((), ())), preferred_element_type=jnp.float32
    )


def rearrange(inputs, moves, out_shapes, scalars):
    def aligned(place, tile):
        return (place[1] if isinstance(place, tuple) else place) % tile == 0

    if all(
        aligned(value, tile)
        for move in moves
        for value, tile in zip(move[1:3] + move[4:8], (16, 128) * 3)
    ):
        tables = jnp.stack([jnp.asarray(s, jnp.int32) for s in scalars])

        def kernel(table, *refs):
            sources, targets, sems = refs[: len(inputs)], refs[len(inputs) : -1], refs[-1]

            def place(value, tile):
                if isinstance(value, tuple):
                    return pl.multiple_of(table[value[0]] * value[1], tile)
                return value

            copies = []
            for i, (a, ar, ac, b, br, bc, rows, columns) in enumerate(moves):
                copies.append(
                    pltpu.make_async_copy(
                        sources[a].at[pl.ds(place(ar, 16), rows), pl.ds(place(ac, 128), columns)],
                        targets[b].at[pl.ds(place(br, 16), rows), pl.ds(place(bc, 128), columns)],
                        sems.at[i],
                    )
                )
                copies[-1].start()
            for copy in copies:
                copy.wait()

        size = sum(r * c for r, c in out_shapes)
        return pl.pallas_call(
            kernel,
            out_shape=[jax.ShapeDtypeStruct(s, jnp.bfloat16) for s in out_shapes],
            in_specs=[pl.BlockSpec(memory_space=pltpu.SMEM)]
            + [pl.BlockSpec(memory_space=pl.ANY)] * len(inputs),
            out_specs=[pl.BlockSpec(memory_space=pltpu.VMEM)] * len(out_shapes),
            scratch_shapes=[pltpu.SemaphoreType.DMA((len(moves),))],
            cost_estimate=pl.CostEstimate(flops=0, transcendentals=0, bytes_accessed=4 * size),
        )(tables, *inputs)

    def at(value):
        return scalars[value[0]] * value[1] if isinstance(value, tuple) else value

    outputs = [jnp.zeros(s, jnp.bfloat16) for s in out_shapes]
    for a, ar, ac, b, br, bc, rows, columns in moves:
        block = lax.dynamic_slice(inputs[a], (at(ar), at(ac)), (rows, columns))
        outputs[b] = lax.dynamic_update_slice(outputs[b], block, (at(br), at(bc)))
    return outputs


def add(*terms):
    return sum(t.astype(jnp.float32) for t in terms).astype(jnp.bfloat16)


def body(n_dp, n_mp):
    n_chips = n_mp // 2
    if n_chips != n_dp or n_dp & (n_dp - 1) or n_dp < 4:
        raise ValueError("mesh shape")
    places = range(n_dp)

    def move(value, dz, dm):
        pairs = [
            (z * n_mp + m, (z ^ dz) * n_mp + (m ^ dm)) for z in range(n_dp) for m in range(n_mp)
        ]
        return lax.ppermute(value, ("dp", "mp"), pairs)

    z_masks = []
    span = n_dp
    while span > 1:
        z_masks.append(span - 1)
        span //= 2
    near = [0]
    for mask in z_masks[:-1]:
        near += [j ^ mask for j in near]
    groups = [[j ^ z_masks[-1] for j in near], near]
    bits = [1 << i for i in range(n_chips.bit_length() - 1)]

    def gather_z(own):
        blocks = {0: own}
        for mask in z_masks:
            blocks.update({j ^ mask: move(b, mask, 0) for j, b in list(blocks.items())})
        return blocks

    def reduce_z(blocks):
        blocks = dict(blocks)
        for i in reversed(range(len(z_masks))):
            kept = [0]
            for earlier in z_masks[:i]:
                kept += [j ^ earlier for j in kept]
            arrived = {}
            for j in kept:
                far = j ^ z_masks[i]
                arrived[j] = move(blocks.pop(far), z_masks[i], 0)
            for j in kept:
                blocks[j] = add(blocks[j], arrived[j])
        return blocks[0]

    def gather_chips(own):
        half, width = own.shape[0] // 2, own.shape[1]
        a = move(own, 0, 2 * bits[0])
        b = move(own, 0, 2 * bits[1])
        upper, lower = rearrange(
            [a, b],
            [(0, 0, 0, 0, 0, 0, half, width), (1, half, 0, 1, 0, 0, half, width)],
            [(half, width)] * 2,
            [0],
        )
        upper = move(upper, 0, 2 * bits[1])
        lower = move(lower, 0, 2 * bits[0])
        known = [(0, 0, own), (1, 0, a), (2, 0, b), (3, 0, upper), (3, half, lower)]
        for bit in bits[2:]:
            known += [(r ^ bit, row, move(x, 0, 2 * bit)) for r, row, x in known]
        return known

    def reduce_chips(blocks, parts):
        blocks = dict(blocks)
        for bit in reversed(bits[2:]):
            for r, row in [k for k in blocks if k[0] & bit]:
                arrived = move(blocks.pop((r, row)), 0, 2 * bit)
                blocks[r ^ bit, row] = add(blocks[r ^ bit, row], arrived)
        half = blocks[0, 0].shape[0] // 2
        upper = move(blocks[3, 0], 0, 2 * bits[0])
        lower = move(blocks[3, 1], 0, 2 * bits[1])
        to_b = jnp.concatenate([add(blocks[2, 0][:half], upper), blocks[2, 0][half:]])
        from_b = move(to_b, 0, 2 * bits[1])
        to_a = jnp.concatenate([blocks[1, 0][:half], add(blocks[1, 0][half:], lower)])
        from_a = move(to_a, 0, 2 * bits[0])
        rows = 2 * half // parts
        return [
            add(*(x[i * rows : (i + 1) * rows] for x in (blocks[0, 0], from_a, from_b)))
            for i in range(parts)
        ]

    def shards(tokens, w_first, w_second, cotangent):
        z, m = lax.axis_index("dp"), lax.axis_index("mp")
        core = m & 1
        shift = z ^ (m >> 1)
        rows, width = tokens.shape
        units = w_first.shape[1] // n_dp
        features = n_chips * width
        by_z = [z ^ j for j in places]
        by_shift = [shift ^ j for j in places]
        scalars = [core, 1 - core] + by_z + by_shift
        z_at, shift_at = 2, 2 + n_dp

        def spread(array, unit_dim):
            def turned(pair):
                return pair if unit_dim == 1 else pair[::-1]

            def moved(a, source, b, target, size):
                return (a, *turned(source), b, *turned(target), *turned(size))

            other = lax.dynamic_slice(
                array, turned(((1 - core) * width, 0)), turned((width, n_dp * units))
            )
            other = move(other, 0, 1)
            parts = rearrange(
                [array, other],
                [
                    moved(c, (((0, width), 0)[c], (z_at + j, units)), j, (0, c * units), (width, units))
                    for j in places
                    for c in range(2)
                ],
                [turned((width, 2 * units))] * n_dp,
                scalars,
            )
            parts = [parts[0]] + [move(parts[j], j, 0) for j in places if j]
            return rearrange(
                parts,
                [
                    moved(j, (0, 0), 0, ((shift_at + j, width), 0), (width, 2 * units))
                    for j in places
                ],
                [turned((features, 2 * units))],
                scalars,
            )[0]

        def unspread(array, unit_dim):
            def turned(pair):
                return pair if unit_dim == 1 else pair[::-1]

            def moved(a, source, b, target, size):
                return (a, *turned(source), b, *turned(target), *turned(size))

            other = move(lax.slice(array, turned((0, units)), turned((features, 2 * units))), 0, 1)
            parts = rearrange(
                [array, other],
                [
                    moved(c, ((shift_at + j, width), 0), j, ((c, width), 0), (width, units))
                    for j in places
                    for c in range(2)
                ],
                [turned((2 * width, units))] * n_dp,
                scalars,
            )
            result = jnp.zeros(turned((2 * width, n_dp * units)), jnp.float32)
            for j in (0, *reversed(places[1:])):
                part = move(parts[j], j, 0) if j else parts[j]
                result = lax.dynamic_update_slice(
                    result, part.astype(jnp.float32), turned((0, by_z[j] * units))
                )
            return result

        def gather(own):
            known = gather_z(own)
            blocks, moves = [], []
            for g in (1, 0):
                size = len(groups[g])
                joined = rearrange(
                    [known[j] for j in groups[g]],
                    [(i, 0, 0, 0, i * rows, 0, rows, width) for i in range(size)],
                    [(size * rows, width)],
                    [0],
                )[0]
                for r, row, block in gather_chips(joined):
                    moves.append(
                        (len(blocks), 0, 0, 0, g * size * rows + row, r * width, block.shape[0], width)
                    )
                    blocks.append(block)
            return rearrange(blocks, moves, [(n_dp * rows, features)], [0])[0]

        def reduce(share):
            size = n_dp * rows // 2
            keys, moves, shapes = [], [], []
            for g in range(2):
                for r in range(n_chips):
                    for row in range(2) if r & 3 == 3 else range(1):
                        count = size // 2 if r & 3 == 3 else size
                        moves.append(
                            (0, g * size + row * count, r * width, len(keys), 0, 0, count, width)
                        )
                        keys.append((g, r, row))
                        shapes.append((count, width))
            blocks = dict(zip(keys, rearrange([share], moves, shapes, [0])))
            known = {}
            for g in range(2):
                mine = {k[1:]: v for k, v in blocks.items() if k[0] == g}
                known.update(zip(groups[g], reduce_chips(mine, len(groups[g]))))
            return reduce_z(known)

        def over_cores(share):
            return share[:, :units] + move(share[:, units:], 0, 1)

        def both(half):
            return jnp.concatenate([half, move(half, 0, 1)], axis=1)

        inputs_all = gather(tokens)
        first = spread(w_first, 1)
        piece = gather(cotangent)
        second = spread(w_second, 0)
        share = product(inputs_all, first, 1, 0)
        pre_act = over_cores(share)
        half = gelu_value(pre_act).astype(jnp.bfloat16)
        half, slope = lax.optimization_barrier((half, gelu_slope(pre_act)))
        activated = both(half)
        second_terms = product(activated, piece, 0, 0).astype(jnp.bfloat16)
        second_grad = unspread(second_terms, 0)
        share = product(activated, second, 1, 0).astype(jnp.bfloat16)
        outputs = reduce(share)
        share = product(piece, second, 1, 1)
        back_pre = over_cores(share)
        half = (back_pre * slope).astype(jnp.bfloat16)
        hidden_grad = both(half)
        first_terms = product(inputs_all, hidden_grad, 0, 0).astype(jnp.bfloat16)
        first_grad = unspread(first_terms, 1)
        share = product(hidden_grad, first, 1, 1).astype(jnp.bfloat16)
        input_grad = reduce(share)
        return (outputs, input_grad, first_grad, second_grad)

    return shards


def solution(mesh):
    return jax.shard_map(
        body(mesh.shape["dp"], mesh.shape["mp"]),
        mesh=mesh,
        in_specs=(P("dp", "mp"), P("dp", "mp"), P("mp", "dp"), P("dp", "mp")),
        out_specs=(P("dp", "mp"), P("dp", "mp"), P("dp", "mp"), P("mp", "dp")),
        check_vma=False,
    )
```
